32 devices in a mesh: groups: 2 (over y), seq: 4 (over x, core), heads: 4 (over z).
Axes of the slice: x: 2, y: 2, z: 4, core: 2. Of those that a mesh axis runs over, the one named last changes fastest.
Arguments:
- tokens: bfloat16 [4096, 8192], P(('groups', 'seq'), 'heads'), parts along dimension 0, may hold values from -6 to 6
- xz_weight: bfloat16 [8192, 32768], P(None, ('heads', 'seq')), may hold values from -0.0625 to 0.0625
- bc_weight: bfloat16 [8192, 2048], P(None, 'heads'), may hold values from -0.0625 to 0.0625
- step_weight: bfloat16 [8192, 256], P(None, 'heads'), may hold values from -0.0625 to 0.0625
- step_bias: float32 [256], P('heads'), may hold values from -4 to -2
- decay_log: float32 [256], P('heads'), may hold values from -5.3 to -0.7
- skip_gain: float32 [256], P('heads'), may hold values from 0.5 to 2
- conv_weight: float32 [4, 16384], P(None, 'heads'), may hold values from -3 to 3
- conv_bias: float32 [16384], P('heads'), may hold values from -3 to 3
- bc_conv_weight: float32 [4, 2048], replicated, may hold values from -3 to 3
- bc_conv_bias: float32 [2048], replicated, may hold values from -3 to 3
- norm_gain: float32 [16384], P('heads'), may hold values from 0.1 to 1.9
- step_bounds: int32 [32], P('groups'), parts along dimension 0, may hold values from 0 to 2047, as said below
- readers: int32 [32], P('groups'), parts along dimension 0, may hold values from 0 to 3, as said below
Outputs:
- mixed: bfloat16 [4096, 16384], P(('groups', 'seq'), 'heads'), parts along dimension 0
- handoff: bfloat16 [8, 4, 256, 64, 128], P(('groups', 'heads'), None, 'seq'), parts along dimension 0
The draws below stay inside these ranges and needn't reach their ends.
There are 2 independent parts, one for each index of `groups`. The reference program is written for one: setup_inputs(seed, part) draws one part's arguments, and reference() takes and returns one part's arrays. A program takes and returns all parts, laid end to end along the dimension named above; an argument that names none is the same for every part. Nothing has to cross between parts.
Inputs may be any that keep to these rules, and one draw needn't show every extreme that they name: `step_bounds`: boundary j * 4 + i, for i < 4, lies in section j: positions j * 512 to (j + 1) * 512 - 1. The first boundary is at position 0 and the last at 2047. `readers`: among the 4 boundaries of each section every reader appears exactly once.
All inputs are finite; a program needn't handle non-finite values.
Results may differ from the reference program's by a relative error of at most 0.0056.
Values may be sent and summed in bfloat16 or wider, within the bound.
A program may use at most 384 MiB of HBM per device.

```python
import jax
import jax.numpy as jnp
from jax import lax

D = 8192
H = 256
P_SIZE = 64
N = 128
G = 8
K = 4
CH = 256
SEC = 512
TRACE = 2048
READERS = 4
BOUNDS = 16


def draw_step_bounds(key, part):
    sections = BOUNDS // READERS
    offsets = jax.random.randint(jax.random.fold_in(key, 11), (sections, READERS), 0, SEC).astype(jnp.int32)
    offsets = offsets.at[0, 0].set(0)
    offsets = offsets.at[sections - 1, READERS - 1].set(SEC - 1)
    section_starts = (jnp.arange(sections, dtype=jnp.int32) * SEC)[:, None]
    return (offsets + section_starts).reshape(BOUNDS).astype(jnp.int32)


def draw_readers(key, part):
    sections = BOUNDS // READERS
    section_keys = jax.random.split(jax.random.fold_in(key, 23), sections)
    assignment = jax.vmap(lambda one_key: jax.random.permutation(one_key, READERS))(section_keys)
    return assignment.reshape(BOUNDS).astype(jnp.int32)


def levels(own_key, shape, cuts, low, top_value):
    level = 1.0
    for dim, blocks in cuts:
        steps = jax.random.uniform(jax.random.fold_in(jax.random.fold_in(own_key, 6), dim), (blocks,), jnp.float32, low / len(cuts), top_value / len(cuts))
        level = level * jnp.repeat(jnp.exp(steps), shape[dim] // blocks).reshape((-1,) + (1,) * (len(shape) - 1 - dim))
    return level


def bell_draw(own_key, shape, scale, reach, cuts=(), kind=jnp.bfloat16):
    result = scale * jax.random.normal(own_key, shape, jnp.float32)
    if cuts:
        result = result * levels(own_key, shape, cuts, -0.22, 0.18)
    return jnp.clip(result, -reach, reach).astype(kind)


def setup_inputs(seed: int = 0, part: int = 0) -> dict:
    keys = jax.random.split(jax.random.key(seed), 15)
    part_keys = jax.random.split(jax.random.fold_in(keys[14], part), 15)
    tokens = bell_draw(part_keys[0], (TRACE, D), 1.0, 6.0, ((0, 4), (1, 4)))
    xz_weight = bell_draw(keys[1], (D, H * 2 * P_SIZE), D ** -0.5, 0.0625, ((1, 16),))
    bc_weight = bell_draw(keys[2], (D, G * 2 * N), D ** -0.5, 0.0625, ((1, 4),))
    step_weight = bell_draw(keys[3], (D, H), D ** -0.5, 0.0625, ((1, 4),))
    step_bias = jnp.clip(-4.0 + 2.0 * jax.random.uniform(keys[4], (H,), jnp.float32) ** levels(keys[4], (H,), ((0, 4),), -0.2, 0.2), -4.0, -2.0)
    decay_log = jnp.clip(-5.3 + 4.6000002 * jax.random.uniform(keys[5], (H,), jnp.float32) ** levels(keys[5], (H,), ((0, 4),), -0.2, 0.2), -5.3, -0.7)
    skip_gain = jnp.clip(0.5 + 1.5 * jax.random.uniform(keys[6], (H,), jnp.float32) ** levels(keys[6], (H,), ((0, 4),), -0.2, 0.2), 0.5, 2.0)
    conv_weight = bell_draw(keys[7], (K, H * P_SIZE), K ** -0.5, 3.0, ((1, 4),), jnp.float32)
    conv_bias = bell_draw(keys[8], (H * P_SIZE,), 0.5, 3.0, ((0, 4),), jnp.float32)
    bc_conv_weight = bell_draw(keys[9], (K, G * 2 * N), K ** -0.5, 3.0, (), jnp.float32)
    bc_conv_bias = bell_draw(keys[10], (G * 2 * N,), 0.5, 3.0, (), jnp.float32)
    norm_gain = jnp.clip(1.0 + 0.18 * jax.random.normal(keys[11], (H * P_SIZE,), jnp.float32), 0.1, 1.9)
    step_bounds = draw_step_bounds(jax.random.fold_in(jax.random.fold_in(keys[14], part), 71), part)
    readers = draw_readers(jax.random.fold_in(jax.random.fold_in(keys[14], part), 71), part)
    return {"tokens": tokens, "xz_weight": xz_weight, "bc_weight": bc_weight, "step_weight": step_weight, "step_bias": step_bias, "decay_log": decay_log, "skip_gain": skip_gain, "conv_weight": conv_weight, "conv_bias": conv_bias, "bc_conv_weight": bc_conv_weight, "bc_conv_bias": bc_conv_bias, "norm_gain": norm_gain, "step_bounds": step_bounds, "readers": readers}


EPSILON = 1e-05
HIGHEST_PRECISION = lax.Precision.HIGHEST

def conv_rows(prefix, raw_rows, kernel, shift_bias):
    row_count = raw_rows.shape[0]
    padded = jnp.concatenate([prefix, raw_rows], axis=0).astype(jnp.float32)
    summed = jnp.broadcast_to(shift_bias[None, :], raw_rows.shape)
    for tap_index in range(kernel.shape[0]):
        summed = summed + kernel[tap_index][None, :] * padded[tap_index:tap_index + row_count]
    return jax.nn.silu(summed).astype(jnp.bfloat16)

def reference(tokens, xz_weight, bc_weight, step_weight, step_bias, decay_log, skip_gain, conv_weight, conv_bias, bc_conv_weight, bc_conv_bias, norm_gain, step_bounds, readers):
    length = tokens.shape[0]
    per_group = H // G
    taps = conv_weight.shape[0]
    xz_rows = jnp.dot(tokens, xz_weight, preferred_element_type=jnp.float32).astype(jnp.bfloat16).reshape(length, H, 2 * P_SIZE)
    inner_raw = xz_rows[:, :, :P_SIZE].reshape(length, H * P_SIZE)
    gate_raw = xz_rows[:, :, P_SIZE:].reshape(length, G, per_group, P_SIZE)
    bc_raw = jnp.dot(tokens, bc_weight, preferred_element_type=jnp.float32).astype(jnp.bfloat16)
    step_size = jax.nn.softplus(jnp.dot(tokens, step_weight, preferred_element_type=jnp.float32) + step_bias[None, :]).reshape(length, G, per_group)
    decay_rate = -jnp.exp(decay_log).reshape(G, per_group)[None] * step_size
    inner_conv = conv_rows(jnp.zeros((taps - 1, H * P_SIZE), jnp.bfloat16), inner_raw, conv_weight, conv_bias).reshape(length, G, per_group, P_SIZE)
    bc_conv = conv_rows(jnp.zeros((taps - 1, G * 2 * N), jnp.bfloat16), bc_raw, bc_conv_weight, bc_conv_bias).reshape(length, G, 2 * N)
    b_input = bc_conv[:, :, :N]
    c_input = bc_conv[:, :, N:]
    blocks = length // CH
    inner_blocks = inner_conv.reshape(blocks, CH, G, per_group, P_SIZE)
    b_blocks = b_input.reshape(blocks, CH, G, N)
    c_blocks = c_input.reshape(blocks, CH, G, N)
    step_blocks = step_size.reshape(blocks, CH, G, per_group)
    cum_blocks = jnp.cumsum(decay_rate.reshape(blocks, CH, G, per_group), axis=1)
    causal = lax.broadcasted_iota(jnp.int32, (CH, CH), 0) >= lax.broadcasted_iota(jnp.int32, (CH, CH), 1)

    def block_step(running, pieces):
        inner_blk, b_blk, c_blk, step_blk, cum_block = pieces
        scores = jnp.einsum('tgn,sgn->gts', c_blk.astype(jnp.float32), b_blk.astype(jnp.float32))
        cum_gap = cum_block[:, None] - cum_block[None, :]
        weight = jnp.where(causal[:, :, None, None], jnp.exp(jnp.minimum(cum_gap, 0.0)), 0.0) * step_blk[None]
        mixing = (weight * jnp.transpose(scores, (1, 2, 0))[:, :, :, None]).astype(jnp.bfloat16)
        intra_part = jnp.einsum('tsgr,sgrp->tgrp', mixing.astype(jnp.float32), inner_blk.astype(jnp.float32))
        outer_part = jnp.exp(cum_block)[..., None] * jnp.einsum('tgn,grpn->tgrp', c_blk.astype(jnp.float32), running, precision=HIGHEST_PRECISION)
        block_total = cum_block[-1]
        carry_weight = jnp.exp(block_total[None] - cum_block) * step_blk
        weighted = (inner_blk.astype(jnp.float32) * carry_weight[..., None]).astype(jnp.bfloat16)
        new_state = jnp.exp(block_total)[..., None, None] * running + jnp.einsum('sgrp,sgn->grpn', weighted.astype(jnp.float32), b_blk.astype(jnp.float32))
        return (new_state, (intra_part + outer_part, running))
    first_state = jnp.zeros((G, per_group, P_SIZE, N), jnp.float32)
    unused, (ssd_blocks, starts) = lax.scan(block_step, first_state, (inner_blocks, b_blocks, c_blocks, step_blocks, cum_blocks))
    ssd = ssd_blocks.reshape(length, G, per_group, P_SIZE) + skip_gain.reshape(G, per_group)[None, :, :, None] * inner_conv.astype(jnp.float32)
    gated = ssd * jax.nn.silu(gate_raw.astype(jnp.float32))
    square_mean = lax.optimization_barrier(jnp.sum(gated * gated, axis=(2, 3))) / (per_group * P_SIZE)
    normed = gated * lax.rsqrt(square_mean + EPSILON)[:, :, None, None] * norm_gain.reshape(G, per_group, P_SIZE)[None]
    mixed = normed.astype(jnp.bfloat16).reshape(length, H * P_SIZE)
    block_positions = lax.broadcasted_iota(jnp.int32, (CH,), 0)

    def one_bound(position):
        block_index = (position // CH).astype(jnp.int32)
        offset = (position - block_index * CH).astype(jnp.int32)
        inner_blk = lax.dynamic_index_in_dim(inner_blocks, block_index, 0, keepdims=False)
        b_blk = lax.dynamic_index_in_dim(b_blocks, block_index, 0, keepdims=False)
        step_blk = lax.dynamic_index_in_dim(step_blocks, block_index, 0, keepdims=False)
        cum_block = lax.dynamic_index_in_dim(cum_blocks, block_index, 0, keepdims=False)
        start_state = lax.dynamic_index_in_dim(starts, block_index, 0, keepdims=False)
        cum_at = lax.dynamic_index_in_dim(cum_block, offset, 0, keepdims=False)
        weight = jnp.where((block_positions <= offset)[:, None, None], jnp.exp(jnp.minimum(cum_at[None] - cum_block, 0.0)), 0.0) * step_blk
        bound_weighted = (inner_blk.astype(jnp.float32) * weight[..., None]).astype(jnp.bfloat16)
        inside = jnp.einsum('sgrp,sgn->grpn', bound_weighted.astype(jnp.float32), b_blk.astype(jnp.float32))
        return (jnp.exp(cum_at)[..., None, None] * start_state + inside).astype(jnp.bfloat16)
    states = lax.map(one_bound, step_bounds)
    sections = step_bounds.shape[0] // READERS
    states = states.reshape(sections, READERS, H, P_SIZE, N)
    order = jnp.argsort(readers.reshape(sections, READERS), axis=1).astype(jnp.int32)
    ordered = jnp.take_along_axis(states, order[:, :, None, None, None], axis=1)
    handoff = jnp.transpose(ordered, (1, 0, 2, 3, 4))
    return (mixed, handoff)
```

```python
import jax
import jax.numpy as jnp
from jax import lax
from jax.sharding import PartitionSpec as P

H = 256
P_SIZE = 64
N = 128
G = 8
CH = 256
PER_GROUP = H // G
EPSILON = 1e-05


def conv_rows(raw_rows, kernel, shift_bias):
    row_count = raw_rows.shape[0]
    taps = kernel.shape[0]
    padded = jnp.pad(raw_rows, ((taps - 1, 0), (0, 0))).astype(jnp.float32)
    summed = jnp.broadcast_to(shift_bias[None, :], raw_rows.shape)
    for tap_index in range(taps):
        summed = summed + kernel[tap_index][None, :] * padded[tap_index : tap_index + row_count]
    return jax.nn.silu(summed).astype(jnp.bfloat16)


def project(tokens, xz_weight, bc_weight, step_weight, chunks):
    rows = tokens.shape[0] // chunks
    xz, bc, step = [], [], []
    for c in range(chunks):
        part = lax.all_gather(tokens[c * rows : (c + 1) * rows], "heads", axis=1, tiled=True)
        part = lax.all_gather(part, "seq", axis=0)
        dot = lambda w: lax.dot_general(
            part, w, (((2,), (0,)), ((), ())), preferred_element_type=jnp.float32
        )
        xz.append(dot(xz_weight).astype(jnp.bfloat16))
        bc.append(dot(bc_weight).astype(jnp.bfloat16))
        step.append(dot(step_weight))
    whole = lambda parts: jnp.stack(parts, axis=1).reshape(-1, parts[0].shape[-1])
    return whole(xz), whole(bc), whole(step)


def shards(
    tokens,
    xz_weight,
    bc_weight,
    step_weight,
    step_bias,
    decay_log,
    skip_gain,
    conv_weight,
    conv_bias,
    bc_conv_weight,
    bc_conv_bias,
    norm_gain,
    step_bounds,
    readers,
):
    head_devices = lax.axis_size("heads")
    sections = lax.axis_size("seq")
    section = lax.axis_index("seq")
    head_block = lax.axis_index("heads")
    block_heads = H // head_devices
    mine = block_heads // sections
    first_mine = section * mine
    group = (head_block * block_heads + first_mine) // PER_GROUP
    own = lambda a, width, axis: lax.dynamic_slice_in_dim(a, first_mine * width, mine * width, axis)
    width_bc = bc_weight.shape[1]
    whole_group = width_bc >= 2 * N
    if whole_group:
        first_col = group * 2 * N - head_block * width_bc
        bc_weight = lax.dynamic_slice_in_dim(bc_weight, first_col, 2 * N, 1)
    xz, bc_raw, step_raw = project(
        tokens, xz_weight, bc_weight, own(step_weight, 1, 1), 4
    )
    if not whole_group:
        bc_raw = lax.all_gather(bc_raw, "heads", axis=1, tiled=True)
        bc_raw = lax.dynamic_slice_in_dim(bc_raw, group * 2 * N, 2 * N, 1)
    length = xz.shape[0]
    blocks = length // CH
    xz = xz.reshape(length, mine, 2, P_SIZE)
    inner_raw = xz[:, :, 0].reshape(length, mine * P_SIZE)
    gate_raw = xz[:, :, 1]
    inner = conv_rows(inner_raw, own(conv_weight, P_SIZE, 1), own(conv_bias, P_SIZE, 0)).reshape(
        blocks, CH, mine, P_SIZE
    )
    bc = conv_rows(
        bc_raw,
        lax.dynamic_slice_in_dim(bc_conv_weight, group * 2 * N, 2 * N, 1),
        lax.dynamic_slice_in_dim(bc_conv_bias, group * 2 * N, 2 * N, 0),
    ).reshape(blocks, CH, 2 * N)
    b_input, c_input = bc[:, :, :N], bc[:, :, N:]
    step_size = jax.nn.softplus(step_raw + own(step_bias, 1, 0)[None]).reshape(blocks, CH, mine)
    decay = -jnp.exp(own(decay_log, 1, 0))[None, None] * step_size
    cum = jnp.cumsum(decay, axis=1)
    total = cum[:, -1]
    causal = lax.broadcasted_iota(jnp.int32, (CH, CH), 0) >= lax.broadcasted_iota(
        jnp.int32, (CH, CH), 1
    )
    carry_weight = jnp.exp(total[:, None] - cum) * step_size
    inner_f = inner.astype(jnp.float32)
    weighted = (inner_f * carry_weight[..., None]).astype(jnp.bfloat16)
    added = jnp.einsum("cshp,csn->chpn", weighted, b_input, preferred_element_type=jnp.float32)
    starts = [jnp.zeros_like(added[0])]
    for c in range(blocks - 1):
        starts.append(jnp.exp(total[c])[:, None, None] * starts[-1] + added[c])
    starts = jnp.stack(starts)
    scores = jnp.einsum("ctn,csn->cts", c_input, b_input, preferred_element_type=jnp.float32)
    cum_h = jnp.transpose(cum, (0, 2, 1))
    step_h = jnp.transpose(step_size, (0, 2, 1))
    gap = cum_h[:, :, :, None] - cum_h[:, :, None, :]
    mixing = (
        jnp.where(causal, jnp.exp(jnp.minimum(gap, 0.0)), 0.0)
        * step_h[:, :, None, :]
        * scores[:, None]
    ).astype(jnp.bfloat16)
    intra = jnp.einsum("chts,cshp->cthp", mixing, inner, preferred_element_type=jnp.float32)
    outer = jnp.exp(cum)[..., None] * jnp.einsum(
        "ctn,chpn->cthp", c_input, starts.astype(jnp.bfloat16), preferred_element_type=jnp.float32
    )
    ssd = intra + outer + own(skip_gain, 1, 0)[:, None] * inner_f
    gated = ssd.reshape(length, mine, P_SIZE) * jax.nn.silu(gate_raw.astype(jnp.float32))

    bounds_per = step_bounds.shape[0] // sections
    order = jnp.argsort(readers.reshape(sections, bounds_per), axis=1)
    ordered = jnp.take_along_axis(step_bounds.reshape(sections, bounds_per), order, axis=1)
    positions = jnp.transpose(ordered).reshape(-1)
    block_of = positions // CH
    offset = positions % CH
    cum_b = cum[block_of]
    cum_at = jnp.take_along_axis(cum_b, offset[:, None, None], axis=1)
    inside_mask = lax.broadcasted_iota(jnp.int32, (1, CH), 1) <= offset[:, None]
    bound_weight = (
        jnp.where(inside_mask[:, :, None], jnp.exp(jnp.minimum(cum_at - cum_b, 0.0)), 0.0)
        * step_size[block_of]
    )
    bound_weighted = (inner_f[block_of] * bound_weight[..., None]).astype(jnp.bfloat16)
    inside = jnp.einsum(
        "bshp,bsn->bhpn", bound_weighted, b_input[block_of], preferred_element_type=jnp.float32
    )
    states = jnp.exp(cum_at[:, 0])[..., None, None] * starts[block_of] + inside
    states = states.astype(jnp.bfloat16).reshape(bounds_per, sections, mine, P_SIZE, N)

    sub = head_devices // sections
    rank = section * sub + head_block % sub
    pieces = []
    for d in range(head_devices):
        pairs = [
            (s * head_devices + k, (k // sub) * head_devices + (s * sub + k % sub + d) % head_devices)
            for s in range(sections)
            for k in range(head_devices)
        ]
        piece = lax.dynamic_index_in_dim(states, (rank + d) % head_devices, 0, False)
        pieces.append(lax.ppermute(piece, ("seq", "heads"), pairs))
    stacked = jnp.stack(pieces)
    source = jnp.arange(head_devices)
    by_rank = jnp.take(stacked, (head_block - source) % head_devices, axis=0)
    by_rank = by_rank.reshape(sections, sub, sections, mine, P_SIZE, N)
    handoff = jnp.transpose(by_rank, (2, 1, 0, 3, 4, 5)).reshape(
        1, sections, sub * sections * mine, P_SIZE, N
    )

    gated = gated.astype(jnp.bfloat16).reshape(length, mine * P_SIZE)
    gated = lax.all_to_all(gated, "seq", split_axis=0, concat_axis=1, tiled=True)
    gated = gated.astype(jnp.float32)
    row_count = gated.shape[0]
    local_groups = max(1, block_heads // PER_GROUP)
    square = jnp.sum(jnp.square(gated.reshape(row_count, local_groups, -1)), axis=2)
    if block_heads < PER_GROUP:
        first_group = head_block * block_heads // PER_GROUP
        placed = lax.dynamic_update_slice_in_dim(
            jnp.zeros((row_count, G), jnp.float32), square, first_group, 1
        )
        square = lax.dynamic_slice_in_dim(lax.psum(placed, "heads"), first_group, 1, 1)
    scale = lax.rsqrt(square / (PER_GROUP * P_SIZE) + EPSILON)
    normed = gated.reshape(row_count, local_groups, -1) * scale[:, :, None]
    mixed = normed.reshape(row_count, -1) * norm_gain[None]
    return (mixed.astype(jnp.bfloat16), handoff)


def solution(mesh):
    in_specs = (
        P(("groups", "seq"), "heads"),
        P(None, ("heads", "seq")),
        P(None, "heads"),
        P(None, "heads"),
        P("heads"),
        P("heads"),
        P("heads"),
        P(None, "heads"),
        P("heads"),
        P(),
        P(),
        P("heads"),
        P("groups"),
        P("groups"),
    )
    out_specs = (P(("groups", "seq"), "heads"), P(("groups", "heads"), None, "seq", None, None))
    return jax.shard_map(shards, mesh=mesh, in_specs=in_specs, out_specs=out_specs, check_vma=False)
```

```python
import jax
import jax.numpy as jnp
from jax import lax
from jax.sharding import PartitionSpec as P

H = 256
P_SIZE = 64
N = 128
G = 8
CH = 256
PER_GROUP = H // G
EPSILON = 1e-05


def conv_rows(raw_rows, kernel, shift_bias):
    row_count = raw_rows.shape[0]
    taps = kernel.shape[0]
    padded = jnp.pad(raw_rows, ((taps - 1, 0), (0, 0))).astype(jnp.float32)
    summed = jnp.broadcast_to(shift_bias[None, :], raw_rows.shape)
    for tap_index in range(taps):
        summed = summed + kernel[tap_index][None, :] * padded[tap_index : tap_index + row_count]
    return jax.nn.silu(summed).astype(jnp.bfloat16)


def project(tokens, xz_weight, bc_weight, step_weight, chunks):
    sections, head_devices = lax.axis_size("seq"), lax.axis_size("heads")
    rows = tokens.shape[0] // chunks
    width = tokens.shape[1]
    xz, bc, step = [], [], []
    for c in range(chunks):
        part = lax.all_gather(tokens[c * rows : (c + 1) * rows], ("seq", "heads"), axis=0)
        part = part.reshape(sections, head_devices, rows, width)
        dot = lambda w: lax.dot_general(
            part,
            w.reshape(head_devices, width, w.shape[1]),
            (((1, 3), (0, 1)), ((), ())),
            preferred_element_type=jnp.float32,
        )
        xz.append(dot(xz_weight).astype(jnp.bfloat16))
        bc.append(dot(bc_weight).astype(jnp.bfloat16))
        step.append(dot(step_weight))
    whole = lambda parts: jnp.stack(parts, axis=1).reshape(-1, parts[0].shape[-1])
    return whole(xz), whole(bc), whole(step)


def shards(
    tokens,
    xz_weight,
    bc_weight,
    step_weight,
    step_bias,
    decay_log,
    skip_gain,
    conv_weight,
    conv_bias,
    bc_conv_weight,
    bc_conv_bias,
    norm_gain,
    step_bounds,
    readers,
):
    head_devices = lax.axis_size("heads")
    sections = lax.axis_size("seq")
    section = lax.axis_index("seq")
    head_block = lax.axis_index("heads")
    block_heads = H // head_devices
    mine = block_heads // sections
    first_mine = section * mine
    group = (head_block * block_heads + first_mine) // PER_GROUP
    own = lambda a, width, axis: lax.dynamic_slice_in_dim(a, first_mine * width, mine * width, axis)
    width_bc = bc_weight.shape[1]
    whole_group = width_bc >= 2 * N
    if whole_group:
        first_col = group * 2 * N - head_block * width_bc
        bc_weight = lax.dynamic_slice_in_dim(bc_weight, first_col, 2 * N, 1)
    xz, bc_raw, step_raw = project(
        tokens, xz_weight, bc_weight, own(step_weight, 1, 1), 2
    )
    if not whole_group:
        bc_raw = lax.all_gather(bc_raw, "heads", axis=1, tiled=True)
        bc_raw = lax.dynamic_slice_in_dim(bc_raw, group * 2 * N, 2 * N, 1)
    length = xz.shape[0]
    blocks = length // CH
    xz = xz.reshape(length, mine, 2, P_SIZE)
    inner_raw = xz[:, :, 0].reshape(length, mine * P_SIZE)
    gate_raw = xz[:, :, 1]
    inner = conv_rows(inner_raw, own(conv_weight, P_SIZE, 1), own(conv_bias, P_SIZE, 0)).reshape(
        blocks, CH, mine, P_SIZE
    )
    bc = conv_rows(
        bc_raw,
        lax.dynamic_slice_in_dim(bc_conv_weight, group * 2 * N, 2 * N, 1),
        lax.dynamic_slice_in_dim(bc_conv_bias, group * 2 * N, 2 * N, 0),
    ).reshape(blocks, CH, 2 * N)
    b_input, c_input = bc[:, :, :N], bc[:, :, N:]
    step_size = jax.nn.softplus(step_raw + own(step_bias, 1, 0)[None]).reshape(blocks, CH, mine)
    decay = -jnp.exp(own(decay_log, 1, 0))[None, None] * step_size
    cum = jnp.cumsum(decay, axis=1)
    total = cum[:, -1]
    causal = lax.broadcasted_iota(jnp.int32, (CH, CH), 0) >= lax.broadcasted_iota(
        jnp.int32, (CH, CH), 1
    )
    carry_weight = jnp.exp(total[:, None] - cum) * step_size
    inner_f = inner.astype(jnp.float32)
    weighted = (inner_f * carry_weight[..., None]).astype(jnp.bfloat16)
    added = jnp.einsum("cshp,csn->chpn", weighted, b_input, preferred_element_type=jnp.float32)
    starts = [jnp.zeros_like(added[0])]
    for c in range(blocks - 1):
        starts.append(jnp.exp(total[c])[:, None, None] * starts[-1] + added[c])
    starts = jnp.stack(starts)
    bounds_per = step_bounds.shape[0] // sections
    order = jnp.argsort(readers.reshape(sections, bounds_per), axis=1)
    ordered = jnp.take_along_axis(step_bounds.reshape(sections, bounds_per), order, axis=1)
    positions = jnp.transpose(ordered).reshape(-1)
    block_of = positions // CH
    offset = positions % CH
    cum_b = cum[block_of]
    cum_at = jnp.take_along_axis(cum_b, offset[:, None, None], axis=1)
    inside_mask = lax.broadcasted_iota(jnp.int32, (1, CH), 1) <= offset[:, None]
    bound_weight = (
        jnp.where(inside_mask[:, :, None], jnp.exp(jnp.minimum(cum_at - cum_b, 0.0)), 0.0)
        * step_size[block_of]
    )
    bound_weighted = (inner_f[block_of] * bound_weight[..., None]).astype(jnp.bfloat16)
    inside = jnp.einsum(
        "bshp,bsn->bhpn", bound_weighted, b_input[block_of], preferred_element_type=jnp.float32
    )
    states = jnp.exp(cum_at[:, 0])[..., None, None] * starts[block_of] + inside
    states = states.astype(jnp.bfloat16).reshape(bounds_per, sections, mine, P_SIZE, N)
    states, c_input = lax.optimization_barrier((states, c_input))

    scores = jnp.einsum("ctn,csn->cts", c_input, b_input, preferred_element_type=jnp.float32)
    cum_h = jnp.transpose(cum, (0, 2, 1))
    step_h = jnp.transpose(step_size, (0, 2, 1))
    gap = cum_h[:, :, :, None] - cum_h[:, :, None, :]
    mixing = (
        jnp.where(causal, jnp.exp(jnp.minimum(gap, 0.0)), 0.0)
        * step_h[:, :, None, :]
        * scores[:, None]
    ).astype(jnp.bfloat16)
    intra = jnp.einsum("chts,cshp->cthp", mixing, inner, preferred_element_type=jnp.float32)
    outer = jnp.exp(cum)[..., None] * jnp.einsum(
        "ctn,chpn->cthp", c_input, starts.astype(jnp.bfloat16), preferred_element_type=jnp.float32
    )
    ssd = intra + outer + own(skip_gain, 1, 0)[:, None] * inner_f
    gated = ssd.reshape(length, mine, P_SIZE) * jax.nn.silu(gate_raw.astype(jnp.float32))

    sub = head_devices // sections
    rank = section * sub + head_block % sub
    pieces = []
    for d in range(head_devices):
        pairs = [
            (s * head_devices + k, (k // sub) * head_devices + (s * sub + k % sub + d) % head_devices)
            for s in range(sections)
            for k in range(head_devices)
        ]
        piece = lax.dynamic_index_in_dim(states, (rank + d) % head_devices, 0, False)
        pieces.append(lax.ppermute(piece, ("seq", "heads"), pairs))
    stacked = jnp.stack(pieces)
    source = jnp.arange(head_devices)
    by_rank = jnp.take(stacked, (head_block - source) % head_devices, axis=0)
    by_rank = by_rank.reshape(sections, sub, sections, mine, P_SIZE, N)
    handoff = jnp.transpose(by_rank, (2, 1, 0, 3, 4, 5)).reshape(
        1, sections, sub * sections * mine, P_SIZE, N
    )

    gated = gated.astype(jnp.bfloat16).reshape(length, mine * P_SIZE)
    gated = lax.all_to_all(gated, "seq", split_axis=0, concat_axis=1, tiled=True)
    gated = gated.astype(jnp.float32)
    row_count = gated.shape[0]
    local_groups = max(1, block_heads // PER_GROUP)
    square = jnp.sum(jnp.square(gated.reshape(row_count, local_groups, -1)), axis=2)
    if block_heads < PER_GROUP:
        first_group = head_block * block_heads // PER_GROUP
        placed = lax.dynamic_update_slice_in_dim(
            jnp.zeros((row_count, G), jnp.float32), square, first_group, 1
        )
        square = lax.dynamic_slice_in_dim(lax.psum(placed, "heads"), first_group, 1, 1)
    scale = lax.rsqrt(square / (PER_GROUP * P_SIZE) + EPSILON)
    normed = gated.reshape(row_count, local_groups, -1) * scale[:, :, None]
    mixed = normed.reshape(row_count, -1) * norm_gain[None]
    return (mixed.astype(jnp.bfloat16), handoff)


def solution(mesh):
    in_specs = (
        P(("groups", "seq"), "heads"),
        P(None, ("heads", "seq")),
        P(None, "heads"),
        P(None, "heads"),
        P("heads"),
        P("heads"),
        P("heads"),
        P(None, "heads"),
        P("heads"),
        P(),
        P(),
        P("heads"),
        P("groups"),
        P("groups"),
    )
    out_specs = (P(("groups", "seq"), "heads"), P(("groups", "heads"), None, "seq", None, None))
    return jax.shard_map(shards, mesh=mesh, in_specs=in_specs, out_specs=out_specs, check_vma=False)
```

```python
import jax
import jax.numpy as jnp
from jax import lax
from jax.sharding import PartitionSpec as P

H = 256
P_SIZE = 64
N = 128
G = 8
CH = 256
PER_GROUP = H // G
EPSILON = 1e-05


def conv_rows(raw_rows, kernel, shift_bias):
    row_count = raw_rows.shape[0]
    taps = kernel.shape[0]
    padded = jnp.pad(raw_rows, ((taps - 1, 0), (0, 0))).astype(jnp.float32)
    summed = jnp.broadcast_to(shift_bias[None, :], raw_rows.shape)
    for tap_index in range(taps):
        summed = summed + kernel[tap_index][None, :] * padded[tap_index : tap_index + row_count]
    return jax.nn.silu(summed).astype(jnp.bfloat16)


def project(tokens, xz_weight, small_weight, chunks):
    sections, head_devices = lax.axis_size("seq"), lax.axis_size("heads")
    rows = tokens.shape[0] // chunks
    width = tokens.shape[1]
    features = xz_weight.shape[1] // 2
    paired = xz_weight.reshape(-1, features // P_SIZE, 2, P_SIZE)
    weight = jnp.concatenate(
        [paired[:, :, 0].reshape(-1, features), paired[:, :, 1].reshape(-1, features)], axis=1
    )
    pieces = [tokens[c * rows : (c + 1) * rows] for c in range(chunks)]
    xz, small = [], []
    for c in range(chunks):
        part = lax.all_gather(pieces[c], ("seq", "heads"), axis=0)
        part = part.reshape(sections, head_devices, rows, width)
        dot = lambda w: lax.dot_general(
            part,
            w.reshape(head_devices, width, w.shape[1]),
            (((1, 3), (0, 1)), ((), ())),
            preferred_element_type=jnp.float32,
        )
        xz.append(dot(weight).astype(jnp.bfloat16))
        small.append(dot(small_weight))
        if c + 2 < chunks:
            pieces[c + 2], xz[c], small[c] = lax.optimization_barrier(
                (pieces[c + 2], xz[c], small[c])
            )
    whole = lambda parts: jnp.concatenate(parts, axis=1).reshape(-1, parts[0].shape[-1])
    return whole([p[..., :features] for p in xz]), whole([p[..., features:] for p in xz]), whole(small)


def shards(
    tokens,
    xz_weight,
    bc_weight,
    step_weight,
    step_bias,
    decay_log,
    skip_gain,
    conv_weight,
    conv_bias,
    bc_conv_weight,
    bc_conv_bias,
    norm_gain,
    step_bounds,
    readers,
):
    head_devices = lax.axis_size("heads")
    sections = lax.axis_size("seq")
    section = lax.axis_index("seq")
    head_block = lax.axis_index("heads")
    block_heads = H // head_devices
    mine = block_heads // sections
    first_mine = section * mine
    group = (head_block * block_heads + first_mine) // PER_GROUP
    own = lambda a, width, axis: lax.dynamic_slice_in_dim(a, first_mine * width, mine * width, axis)
    width_bc = bc_weight.shape[1]
    whole_group = width_bc >= 2 * N
    if whole_group:
        first_col = group * 2 * N - head_block * width_bc
        bc_weight = lax.dynamic_slice_in_dim(bc_weight, first_col, 2 * N, 1)
    bc_width = bc_weight.shape[1]
    small_weight = jnp.concatenate([bc_weight, own(step_weight, 1, 1)], axis=1)
    inner_raw, gate_raw, small = project(tokens, xz_weight, small_weight, 4)
    bc_raw = small[:, :bc_width].astype(jnp.bfloat16)
    step_raw = small[:, bc_width:]
    if not whole_group:
        bc_raw = lax.all_gather(bc_raw, "heads", axis=1, tiled=True)
        bc_raw = lax.dynamic_slice_in_dim(bc_raw, group * 2 * N, 2 * N, 1)
    length = inner_raw.shape[0]
    blocks = length // CH
    inner = conv_rows(inner_raw, own(conv_weight, P_SIZE, 1), own(conv_bias, P_SIZE, 0)).reshape(
        blocks, CH, mine, P_SIZE
    )
    bc = conv_rows(
        bc_raw,
        lax.dynamic_slice_in_dim(bc_conv_weight, group * 2 * N, 2 * N, 1),
        lax.dynamic_slice_in_dim(bc_conv_bias, group * 2 * N, 2 * N, 0),
    ).reshape(blocks, CH, 2 * N)
    b_input, c_input = bc[:, :, :N], bc[:, :, N:]
    step_size = jax.nn.softplus(step_raw + own(step_bias, 1, 0)[None]).reshape(blocks, CH, mine)
    decay = -jnp.exp(own(decay_log, 1, 0))[None, None] * step_size
    cum = jnp.cumsum(decay, axis=1)
    total = cum[:, -1]
    causal = lax.broadcasted_iota(jnp.int32, (CH, CH), 0) >= lax.broadcasted_iota(
        jnp.int32, (CH, CH), 1
    )
    carry_weight = jnp.exp(total[:, None] - cum) * step_size
    inner_f = inner.astype(jnp.float32)
    weighted = (inner_f * carry_weight[..., None]).astype(jnp.bfloat16)
    added = jnp.einsum("cshp,csn->chpn", weighted, b_input, preferred_element_type=jnp.float32)
    starts = [jnp.zeros_like(added[0])]
    for c in range(blocks - 1):
        starts.append(jnp.exp(total[c])[:, None, None] * starts[-1] + added[c])
    starts = jnp.stack(starts)
    bounds_per = step_bounds.shape[0] // sections
    order = jnp.argsort(readers.reshape(sections, bounds_per), axis=1)
    ordered = jnp.take_along_axis(step_bounds.reshape(sections, bounds_per), order, axis=1)
    positions = jnp.transpose(ordered).reshape(-1)
    block_of = positions // CH
    offset = positions % CH
    cum_b = cum[block_of]
    cum_at = jnp.take_along_axis(cum_b, offset[:, None, None], axis=1)
    inside_mask = lax.broadcasted_iota(jnp.int32, (1, CH), 1) <= offset[:, None]
    bound_weight = (
        jnp.where(inside_mask[:, :, None], jnp.exp(jnp.minimum(cum_at - cum_b, 0.0)), 0.0)
        * step_size[block_of]
    )
    bound_weighted = (inner_f[block_of] * bound_weight[..., None]).astype(jnp.bfloat16)
    inside = jnp.einsum(
        "bshp,bsn->bhpn", bound_weighted, b_input[block_of], preferred_element_type=jnp.float32
    )
    states = jnp.exp(cum_at[:, 0])[..., None, None] * starts[block_of] + inside
    states = states.astype(jnp.bfloat16).reshape(bounds_per, sections, mine, P_SIZE, N)
    states, c_input = lax.optimization_barrier((states, c_input))

    scores = jnp.einsum("ctn,csn->cts", c_input, b_input, preferred_element_type=jnp.float32)
    cum_h = jnp.transpose(cum, (0, 2, 1))
    step_h = jnp.transpose(step_size, (0, 2, 1))
    gap = cum_h[:, :, :, None] - cum_h[:, :, None, :]
    mixing = (
        jnp.where(causal, jnp.exp(jnp.minimum(gap, 0.0)), 0.0)
        * step_h[:, :, None, :]
        * scores[:, None]
    ).astype(jnp.bfloat16)
    intra = jnp.einsum("chts,cshp->cthp", mixing, inner, preferred_element_type=jnp.float32)
    outer = jnp.exp(cum)[..., None] * jnp.einsum(
        "ctn,chpn->cthp", c_input, starts.astype(jnp.bfloat16), preferred_element_type=jnp.float32
    )
    ssd = intra + outer + own(skip_gain, 1, 0)[:, None] * inner_f
    gated = ssd.reshape(length, mine * P_SIZE) * jax.nn.silu(gate_raw.astype(jnp.float32))

    sub = head_devices // sections
    rank = section * sub + head_block % sub
    pieces = []
    for d in range(head_devices):
        pairs = [
            (s * head_devices + k, (k // sub) * head_devices + (s * sub + k % sub + d) % head_devices)
            for s in range(sections)
            for k in range(head_devices)
        ]
        piece = lax.dynamic_index_in_dim(states, (rank + d) % head_devices, 0, False)
        pieces.append(lax.ppermute(piece, ("seq", "heads"), pairs))
    stacked = jnp.stack(pieces)
    source = jnp.arange(head_devices)
    by_rank = jnp.take(stacked, (head_block - source) % head_devices, axis=0)
    by_rank = by_rank.reshape(sections, sub, sections, mine, P_SIZE, N)
    handoff = jnp.transpose(by_rank, (2, 1, 0, 3, 4, 5)).reshape(
        1, sections, sub * sections * mine, P_SIZE, N
    )

    gated = gated.astype(jnp.bfloat16)
    gated = lax.all_to_all(gated, "seq", split_axis=0, concat_axis=1, tiled=True)
    gated = gated.astype(jnp.float32)
    row_count = gated.shape[0]
    local_groups = max(1, block_heads // PER_GROUP)
    span = gated.shape[1] // local_groups
    columns = [gated[:, g * span : (g + 1) * span] for g in range(local_groups)]
    square = jnp.stack([jnp.sum(jnp.square(part), axis=1) for part in columns], axis=1)
    if block_heads < PER_GROUP:
        first_group = head_block * block_heads // PER_GROUP
        placed = lax.dynamic_update_slice_in_dim(
            jnp.zeros((row_count, G), jnp.float32), square, first_group, 1
        )
        square = lax.dynamic_slice_in_dim(lax.psum(placed, "heads"), first_group, 1, 1)
    scale = lax.rsqrt(square / (PER_GROUP * P_SIZE) + EPSILON)
    normed = [part * scale[:, g : g + 1] for g, part in enumerate(columns)]
    mixed = jnp.concatenate(normed, axis=1) * norm_gain[None]
    return (mixed.astype(jnp.bfloat16), handoff)


def solution(mesh):
    in_specs = (
        P(("groups", "seq"), "heads"),
        P(None, ("heads", "seq")),
        P(None, "heads"),
        P(None, "heads"),
        P("heads"),
        P("heads"),
        P("heads"),
        P(None, "heads"),
        P("heads"),
        P(),
        P(),
        P("heads"),
        P("groups"),
        P("groups"),
    )
    out_specs = (P(("groups", "seq"), "heads"), P(("groups", "heads"), None, "seq", None, None))
    return jax.shard_map(shards, mesh=mesh, in_specs=in_specs, out_specs=out_specs, check_vma=False)
```
